32 devices in a mesh: seq: 4 (over x, core), ctx: 8 (over z, y).
Axes of the slice: x: 2, y: 2, z: 4, core: 2. Of those that a mesh axis runs over, the one named last changes fastest.
Arguments:
- block_input: bfloat16 [4, 1024, 768], P('seq', 'ctx'), may hold values from -6 to 6
- w_qkv: bfloat16 [768, 2304], P(('seq', 'ctx')), may hold values from -0.21875 to 0.21875
- b_query: bfloat16 [768], P(('seq', 'ctx')), may hold values from -1.5 to 1.5
- b_value: bfloat16 [768], P(('seq', 'ctx')), may hold values from -1.5 to 1.5
- w_out: bfloat16 [768, 768], P(('seq', 'ctx')), may hold values from -4 to 4
- b_out: bfloat16 [768], P(('seq', 'ctx')), may hold values from -1.5 to 1.5
- gain_one: bfloat16 [768], P(('seq', 'ctx')), may hold values from 0.5 to 1.5
- shift_one: bfloat16 [768], P(('seq', 'ctx')), may hold values from -1.5 to 1.5
- gain_two: bfloat16 [768], P(('seq', 'ctx')), may hold values from 0.5 to 1.5
- shift_two: bfloat16 [768], P(('seq', 'ctx')), may hold values from -1.5 to 1.5
- w_up: bfloat16 [768, 3072], P(('seq', 'ctx')), may hold values from -0.21875 to 0.21875
- b_up: bfloat16 [3072], P(('seq', 'ctx')), may hold values from -1.5 to 1.5
- w_down: bfloat16 [3072, 768], P(('seq', 'ctx')), may hold values from -0.109375 to 0.109375
- b_down: bfloat16 [768], P(('seq', 'ctx')), may hold values from -1.5 to 1.5
- cotangent: bfloat16 [4, 1024, 768], P('seq', 'ctx'), may hold values from -6 to 6
Outputs:
- result: bfloat16 [4, 1024, 768], P('seq', 'ctx')
- d_input: float32 [4, 1024, 768], P('seq', 'ctx')
- d_w_qkv: float32 [768, 2304], P(('seq', 'ctx'))
- d_b_query: float32 [768], P(('seq', 'ctx'))
- d_b_value: float32 [768], P(('seq', 'ctx'))
- d_w_out: float32 [768, 768], P(('seq', 'ctx'))
- d_b_out: float32 [768], P(('seq', 'ctx'))
- d_gain_one: float32 [768], P(('seq', 'ctx'))
- d_shift_one: float32 [768], P(('seq', 'ctx'))
- d_gain_two: float32 [768], P(('seq', 'ctx'))
- d_shift_two: float32 [768], P(('seq', 'ctx'))
- d_w_up: float32 [768, 3072], P(('seq', 'ctx'))
- d_b_up: float32 [3072], P(('seq', 'ctx'))
- d_w_down: float32 [3072, 768], P(('seq', 'ctx'))
- d_b_down: float32 [768], P(('seq', 'ctx'))
The draws below stay inside these ranges and needn't reach their ends.
All inputs are finite; a program needn't handle non-finite values.
Results may differ from the reference program's by a relative error of at most 0.012.
Values may be sent and summed in bfloat16 or wider, within the bound.
No kernel may reach another device: no remote copies, remote signals or barrier semaphores. Data moves between devices by JAX's collectives and lax.ppermute only.
A program may use at most 192 MiB of HBM per device.

```python
import math
import jax
import jax.numpy as jnp
from jax import lax

D = 768
HEADS = 12
HD = 64
FF = 3072
SEQLEN = 1024
BATCH = 4


def shard_levels(rng, shape, cuts, low, high):
    level = 1.0
    for dim, shards_of in cuts:
        heights = jax.random.uniform(jax.random.fold_in(jax.random.fold_in(rng, 6), dim), (shards_of,), jnp.float32, low / len(cuts), high / len(cuts))
        level = level * jnp.repeat(jnp.exp(heights), shape[dim] // shards_of).reshape((-1,) + (1,) * (len(shape) - 1 - dim))
    return level


def scatter_about(stream_key, extent, deviation, limit, split=(), kind=jnp.bfloat16):
    drawn = jax.random.normal(stream_key, extent, jnp.float32) * deviation
    if len(split) > 0:
        drawn = shard_levels(stream_key, extent, split, -0.22, 0.18) * drawn
    return jnp.clip(drawn, min=-limit, max=limit).astype(kind)


def setup_inputs(seed: int = 0) -> dict:
    splits = jax.random.split(jax.random.key(seed), 16)
    block_input = scatter_about(splits[0], (BATCH, SEQLEN, D), 1.0, 6.0, ((0, 4), (1, 8)))
    w_qkv = scatter_about(splits[1], (D, 3 * D), D ** -0.5, 0.21875, ((0, 32),))
    b_query = scatter_about(splits[2], (D,), 0.3, 1.5, ((0, 32),))
    b_value = scatter_about(splits[3], (D,), 0.3, 1.5, ((0, 32),))
    w_out = scatter_about(splits[4], (D, D), (HD // 32) ** -0.5, 4.0, ((0, 32),))
    b_out = scatter_about(splits[5], (D,), 0.3, 1.5, ((0, 32),))
    gain_one = jnp.clip(1.0 + 0.1 * jax.random.normal(splits[6], (D,), jnp.float32), 0.5, 1.5).astype(jnp.bfloat16)
    shift_one = scatter_about(splits[7], (D,), 0.3, 1.5, ((0, 32),))
    gain_two = jnp.clip(1.0 + 0.1 * jax.random.normal(splits[8], (D,), jnp.float32), 0.5, 1.5).astype(jnp.bfloat16)
    shift_two = scatter_about(splits[9], (D,), 0.3, 1.5, ((0, 32),))
    w_up = scatter_about(splits[10], (D, FF), D ** -0.5, 0.21875, ((0, 32),))
    b_up = scatter_about(splits[11], (FF,), 0.3, 1.5, ((0, 32),))
    w_down = scatter_about(splits[12], (FF, D), FF ** -0.5, 0.109375, ((0, 32),))
    b_down = scatter_about(splits[13], (D,), 0.3, 1.5, ((0, 32),))
    cotangent = scatter_about(splits[14], (BATCH, SEQLEN, D), 1.0, 6.0, ((0, 4), (1, 8)))
    return {"block_input": block_input, "w_qkv": w_qkv, "b_query": b_query, "b_value": b_value, "w_out": w_out, "b_out": b_out, "gain_one": gain_one, "shift_one": shift_one, "gain_two": gain_two, "shift_two": shift_two, "w_up": w_up, "b_up": b_up, "w_down": w_down, "b_down": b_down, "cotangent": cotangent}


epsilon = 1e-05
GELU_C = math.sqrt(2.0 / math.pi)

def norm_fwd(inputs, gain, shift):
    row_mean = lax.optimization_barrier(jnp.mean(inputs, -1, keepdims=True))
    centred = inputs - row_mean
    variance = lax.optimization_barrier(jnp.mean(centred * centred, -1, keepdims=True))
    scale = lax.rsqrt(variance + epsilon)
    normed = centred * scale
    return (normed * gain + shift, normed, scale)

def norm_back(upstream, normed, scale, gain):
    scaled = upstream * gain
    grad_in = (scaled - lax.optimization_barrier(jnp.mean(scaled, -1, keepdims=True)) - normed * lax.optimization_barrier(jnp.mean(scaled * normed, -1, keepdims=True))) * scale
    return (grad_in, lax.optimization_barrier(jnp.sum(upstream * normed, 0)), lax.optimization_barrier(jnp.sum(upstream, 0)))

def gelu_fwd(pre_act):
    tangent = jnp.tanh(GELU_C * (pre_act + 0.044715 * pre_act * pre_act * pre_act))
    return 0.5 * pre_act * (1.0 + tangent)

def gelu_grad(pre_act):
    tangent = jnp.tanh(GELU_C * (pre_act + 0.044715 * pre_act * pre_act * pre_act))
    return 0.5 * (1.0 + tangent) + 0.5 * pre_act * (1.0 - tangent * tangent) * GELU_C * (1.0 + 3.0 * 0.044715 * pre_act * pre_act)

def scores_of(query_rows, keys_all, query_pos, key_pos):
    rows_here = query_rows.shape[0]
    length = keys_all.shape[0]
    q_heads = query_rows.astype(jnp.float32).reshape(rows_here, HEADS, HD)
    k_heads = keys_all.astype(jnp.float32).reshape(length, HEADS, HD)
    scores = jnp.einsum('rhd,lhd->hrl', q_heads, k_heads) * 0.125
    causal = key_pos[None, :] <= query_pos[:, None]
    return jnp.where(causal[None], scores, -1e+30)

def attend(query_rows, keys_all, values_all, query_pos, key_pos):
    rows_here = query_rows.shape[0]
    length = keys_all.shape[0]
    scores = scores_of(query_rows, keys_all, query_pos, key_pos)
    row_max = lax.optimization_barrier(jnp.max(scores, -1, keepdims=True))
    log_total = row_max[..., 0] + jnp.log(lax.optimization_barrier(jnp.sum(jnp.exp(scores - row_max), -1)))
    weights = jnp.exp(scores - log_total[..., None]).astype(jnp.bfloat16)
    v_heads = values_all.astype(jnp.float32).reshape(length, HEADS, HD)
    attended = jnp.einsum('hrl,lhd->rhd', weights.astype(jnp.float32), v_heads)
    return (attended.reshape(rows_here, HEADS * HD).astype(jnp.bfloat16), log_total)

def attend_back(query_rows, keys_all, values_all, attended, d_att, log_total, query_pos, key_pos):
    rows_here = query_rows.shape[0]
    length = keys_all.shape[0]
    scores = scores_of(query_rows, keys_all, query_pos, key_pos)
    probs = jnp.exp(scores - log_total[..., None])
    weights = probs.astype(jnp.bfloat16).astype(jnp.float32)
    q_heads = query_rows.astype(jnp.float32).reshape(rows_here, HEADS, HD)
    k_heads = keys_all.astype(jnp.float32).reshape(length, HEADS, HD)
    v_heads = values_all.astype(jnp.float32).reshape(length, HEADS, HD)
    d_heads = d_att.astype(jnp.float32).reshape(rows_here, HEADS, HD)
    o_heads = attended.astype(jnp.float32).reshape(rows_here, HEADS, HD)
    delta = lax.optimization_barrier(jnp.sum(d_heads * o_heads, -1)).T
    d_prob = jnp.einsum('rhd,lhd->hrl', d_heads, v_heads)
    d_score = (0.125 * probs * (d_prob - delta[..., None])).astype(jnp.bfloat16).astype(jnp.float32)
    d_query = jnp.einsum('hrl,lhd->rhd', d_score, k_heads).reshape(rows_here, HEADS * HD)
    d_key = jnp.einsum('hrl,rhd->lhd', d_score, q_heads).reshape(length, HEADS * HD)
    d_value = jnp.einsum('hrl,rhd->lhd', weights, d_heads).reshape(length, HEADS * HD)
    return (d_query, d_key, d_value)

def reference(block_input, w_qkv, b_query, b_value, w_out, b_out, gain_one, shift_one, gain_two, shift_two, w_up, b_up, w_down, b_down, cotangent):
    float_kind = jnp.float32
    brain_kind = jnp.bfloat16
    block_rows = math.gcd(512, SEQLEN)
    block_count = SEQLEN // block_rows
    positions = jnp.arange(SEQLEN, dtype=jnp.int32)

    def per_sequence(totals, item):
        inputs, upstream_b = item
        input_float = inputs.astype(float_kind)
        h_one, n_one, s_one = norm_fwd(input_float, gain_one.astype(float_kind), shift_one.astype(float_kind))
        normed_one = h_one.astype(brain_kind)
        projected = jnp.dot(normed_one, w_qkv, preferred_element_type=float_kind)
        queries = (projected[:, :D] + b_query.astype(float_kind)).astype(brain_kind)
        keys_all = projected[:, D:2 * D].astype(brain_kind)
        values_all = (projected[:, 2 * D:] + b_value.astype(float_kind)).astype(brain_kind)
        q_blocks = queries.reshape(block_count, block_rows, D)
        p_blocks = positions.reshape(block_count, block_rows)
        attended, log_total = lax.map(lambda block: attend(block[0], keys_all, values_all, block[1], positions), (q_blocks, p_blocks))
        attended = attended.reshape(SEQLEN, D)
        mid_stream = input_float + jnp.dot(attended, w_out, preferred_element_type=float_kind) + b_out.astype(float_kind)
        h_two, n_two, s_two = norm_fwd(mid_stream, gain_two.astype(float_kind), shift_two.astype(float_kind))
        normed_two = h_two.astype(brain_kind)
        pre_act = jnp.dot(normed_two, w_up, preferred_element_type=float_kind) + b_up.astype(float_kind)
        hidden = gelu_fwd(pre_act).astype(brain_kind)
        result = mid_stream + jnp.dot(hidden, w_down, preferred_element_type=float_kind) + b_down.astype(float_kind)
        upstream = upstream_b.astype(float_kind)
        d_w_down = jnp.dot(hidden.T, upstream_b, preferred_element_type=float_kind)
        d_b_down = lax.optimization_barrier(jnp.sum(upstream, 0))
        d_hidden = jnp.dot(upstream_b, w_down.T, preferred_element_type=float_kind)
        d_pre = d_hidden * gelu_grad(pre_act)
        d_pre_b = d_pre.astype(brain_kind)
        d_w_up = jnp.dot(normed_two.T, d_pre_b, preferred_element_type=float_kind)
        d_b_up = lax.optimization_barrier(jnp.sum(d_pre, 0))
        d_normed_two = jnp.dot(d_pre_b, w_up.T, preferred_element_type=float_kind)
        d_mid_norm, d_gain_two, d_shift_two = norm_back(d_normed_two, n_two, s_two, gain_two.astype(float_kind))
        d_mid = upstream + d_mid_norm
        d_mid_b = d_mid.astype(brain_kind)
        d_w_out = jnp.dot(attended.T, d_mid_b, preferred_element_type=float_kind)
        d_b_out = lax.optimization_barrier(jnp.sum(d_mid, 0))
        d_att = jnp.dot(d_mid_b, w_out.T, preferred_element_type=float_kind).astype(brain_kind)

        def back_block(carry, block):
            d_query, d_key, d_value = attend_back(block[0], keys_all, values_all, block[1], block[2], block[3], block[4], positions)
            return ((carry[0] + d_key, carry[1] + d_value), d_query)
        zeros_kv = jnp.zeros((SEQLEN, D), float_kind)
        (d_key, d_value), d_query = lax.scan(back_block, (zeros_kv, zeros_kv), (q_blocks, attended.reshape(block_count, block_rows, D), d_att.reshape(block_count, block_rows, D), log_total, p_blocks))
        d_query = d_query.reshape(SEQLEN, D)
        d_proj = jnp.concatenate([d_query, d_key, d_value], 1).astype(brain_kind)
        d_w_qkv = jnp.dot(normed_one.T, d_proj, preferred_element_type=float_kind)
        d_b_query = lax.optimization_barrier(jnp.sum(d_query, 0))
        d_b_value = lax.optimization_barrier(jnp.sum(d_value, 0))
        d_normed_one = jnp.dot(d_proj, w_qkv.T, preferred_element_type=float_kind)
        d_in_norm, d_gain_one, d_shift_one = norm_back(d_normed_one, n_one, s_one, gain_one.astype(float_kind))
        d_input = d_mid + d_in_norm
        grad_terms = (d_w_qkv, d_b_query, d_b_value, d_w_out, d_b_out, d_gain_one, d_shift_one, d_gain_two, d_shift_two, d_w_up, d_b_up, d_w_down, d_b_down)
        totals = jax.tree.map(lambda acc, new: acc + new, totals, grad_terms)
        return (totals, (result.astype(brain_kind), d_input))
    start_totals = (jnp.zeros((D, 3 * D), float_kind), jnp.zeros((D,), float_kind), jnp.zeros((D,), float_kind), jnp.zeros((D, D), float_kind), jnp.zeros((D,), float_kind), jnp.zeros((D,), float_kind), jnp.zeros((D,), float_kind), jnp.zeros((D,), float_kind), jnp.zeros((D,), float_kind), jnp.zeros((D, FF), float_kind), jnp.zeros((FF,), float_kind), jnp.zeros((FF, D), float_kind), jnp.zeros((D,), float_kind))
    totals, (result, d_input) = lax.scan(per_sequence, start_totals, (block_input, cotangent))
    return (result, d_input) + tuple(totals)
```

```python
import math

import jax
import jax.numpy as jnp
from jax import lax
from jax.sharding import PartitionSpec as P

HD = 64


epsilon = 1e-05
GELU_C = math.sqrt(2.0 / math.pi)


def norm_fwd(inputs, gain, shift):
    row_mean = jnp.mean(inputs, -1, keepdims=True)
    centred = inputs - row_mean
    variance = jnp.mean(centred * centred, -1, keepdims=True)
    scale = lax.rsqrt(variance + epsilon)
    normed = centred * scale
    return (normed * gain + shift, normed, scale)


def norm_back(upstream, normed, scale, gain):
    scaled = upstream * gain
    grad_in = (
        scaled
        - jnp.mean(scaled, -1, keepdims=True)
        - normed * jnp.mean(scaled * normed, -1, keepdims=True)
    ) * scale
    return (grad_in, jnp.sum(upstream * normed, 0), jnp.sum(upstream, 0))


def gelu_fwd(pre_act):
    tangent = jnp.tanh(GELU_C * (pre_act + 0.044715 * pre_act * pre_act * pre_act))
    return 0.5 * pre_act * (1.0 + tangent)


def gelu_grad(pre_act):
    tangent = jnp.tanh(GELU_C * (pre_act + 0.044715 * pre_act * pre_act * pre_act))
    return 0.5 * (1.0 + tangent) + 0.5 * pre_act * (1.0 - tangent * tangent) * GELU_C * (
        1.0 + 3.0 * 0.044715 * pre_act * pre_act
    )


def group_scores(q_heads, k_heads, query_pos, key_pos):
    scores = (
        jnp.einsum("rhd,lhd->hrl", q_heads, k_heads, preferred_element_type=jnp.float32) * 0.125
    )
    causal = key_pos[None, :] <= query_pos[:, None]
    return jnp.where(causal[None], scores, -1e30)


def attend_group(queries, keys_all, values_all, query_pos, key_pos):
    rows_here = queries.shape[0]
    length = keys_all.shape[0]
    group_heads = queries.shape[1] // HD
    q_heads = queries.reshape(rows_here, group_heads, HD)
    k_heads = keys_all.reshape(length, group_heads, HD)
    v_heads = values_all.reshape(length, group_heads, HD)
    scores = group_scores(q_heads, k_heads, query_pos, key_pos)
    row_max = jnp.max(scores, -1, keepdims=True)
    log_total = row_max[..., 0] + jnp.log(jnp.sum(jnp.exp(scores - row_max), -1))
    weights = jnp.exp(scores - log_total[..., None]).astype(jnp.bfloat16)
    attended = jnp.einsum("hrl,lhd->rhd", weights, v_heads, preferred_element_type=jnp.float32)
    return (attended.reshape(rows_here, group_heads * HD).astype(jnp.bfloat16), log_total)


def attend_group_back(
    queries, keys_all, values_all, attended, d_att, log_total, query_pos, key_pos
):
    rows_here = queries.shape[0]
    length = keys_all.shape[0]
    group_heads = queries.shape[1] // HD
    q_heads = queries.reshape(rows_here, group_heads, HD)
    k_heads = keys_all.reshape(length, group_heads, HD)
    v_heads = values_all.reshape(length, group_heads, HD)
    d_heads = d_att.reshape(rows_here, group_heads, HD)
    o_heads = attended.reshape(rows_here, group_heads, HD)
    scores = group_scores(q_heads, k_heads, query_pos, key_pos)
    probs = jnp.exp(scores - log_total[..., None])
    weights = probs.astype(jnp.bfloat16)
    delta = jnp.sum(d_heads.astype(jnp.float32) * o_heads.astype(jnp.float32), -1).T
    d_prob = jnp.einsum("rhd,lhd->hrl", d_heads, v_heads, preferred_element_type=jnp.float32)
    d_score = (0.125 * probs * (d_prob - delta[..., None])).astype(jnp.bfloat16)
    d_query = jnp.einsum(
        "hrl,lhd->rhd", d_score, k_heads, preferred_element_type=jnp.float32
    ).reshape(rows_here, group_heads * HD)
    d_key = jnp.einsum(
        "hrl,rhd->lhd", d_score, q_heads, preferred_element_type=jnp.float32
    ).reshape(length, group_heads * HD)
    d_value = jnp.einsum(
        "hrl,rhd->lhd", weights, d_heads, preferred_element_type=jnp.float32
    ).reshape(length, group_heads * HD)
    return (d_query, d_key, d_value)


def general_device(
    block_input,
    w_qkv,
    b_query,
    b_value,
    w_out,
    b_out,
    gain_one,
    shift_one,
    gain_two,
    shift_two,
    w_up,
    b_up,
    w_down,
    b_down,
    cotangent,
):
    float_kind = jnp.float32
    brain_kind = jnp.bfloat16
    row_count = block_input.shape[1]
    width = block_input.shape[2]
    group_width = 4 * HD
    group_count = width // group_width
    gathered = (
        lax.all_gather(w_qkv, ("seq", "ctx"), axis=0, tiled=True),
        lax.all_gather(b_query, ("seq", "ctx"), axis=0, tiled=True),
        lax.all_gather(b_value, ("seq", "ctx"), axis=0, tiled=True),
        lax.all_gather(w_out, ("seq", "ctx"), axis=0, tiled=True),
        lax.all_gather(b_out, ("seq", "ctx"), axis=0, tiled=True),
        lax.all_gather(gain_one, ("seq", "ctx"), axis=0, tiled=True),
        lax.all_gather(shift_one, ("seq", "ctx"), axis=0, tiled=True),
        lax.all_gather(gain_two, ("seq", "ctx"), axis=0, tiled=True),
        lax.all_gather(shift_two, ("seq", "ctx"), axis=0, tiled=True),
        lax.all_gather(w_up, ("seq", "ctx"), axis=0, tiled=True),
        lax.all_gather(b_up, ("seq", "ctx"), axis=0, tiled=True),
        lax.all_gather(w_down, ("seq", "ctx"), axis=0, tiled=True),
        lax.all_gather(b_down, ("seq", "ctx"), axis=0, tiled=True),
    )
    (
        full_qkv,
        full_bq,
        full_bv,
        full_out,
        full_bout,
        full_g1,
        full_s1,
        full_g2,
        full_s2,
        full_up,
        full_bup,
        full_down,
        full_bdown,
    ) = gathered
    input_float = block_input.reshape(row_count, width).astype(float_kind)
    h_one, n_one, s_one = norm_fwd(
        input_float, full_g1.astype(float_kind), full_s1.astype(float_kind)
    )
    normed_one = h_one.astype(brain_kind)
    projected = jnp.dot(normed_one, full_qkv, preferred_element_type=float_kind)
    queries = (projected[:, :width] + full_bq.astype(float_kind)).astype(brain_kind)
    keys_own = projected[:, width : 2 * width].astype(brain_kind)
    values_own = (projected[:, 2 * width :] + full_bv.astype(float_kind)).astype(brain_kind)
    keys_all, values_all = (
        lax.all_gather(keys_own, "ctx", axis=0, tiled=True),
        lax.all_gather(values_own, "ctx", axis=0, tiled=True),
    )
    length = keys_all.shape[0]
    query_pos = lax.axis_index("ctx") * row_count + jnp.arange(row_count, dtype=jnp.int32)
    key_pos = jnp.arange(length, dtype=jnp.int32)
    att_parts = []
    totals_parts = []
    for group in range(group_count):
        lo_col = group * group_width
        hi_col = lo_col + group_width
        piece, log_total = attend_group(
            queries[:, lo_col:hi_col],
            keys_all[:, lo_col:hi_col],
            values_all[:, lo_col:hi_col],
            query_pos,
            key_pos,
        )
        att_parts.append(piece)
        totals_parts.append(log_total)
    attended = jnp.concatenate(att_parts, 1)
    mid_stream = (
        input_float
        + jnp.dot(attended, full_out, preferred_element_type=float_kind)
        + full_bout.astype(float_kind)
    )
    h_two, n_two, s_two = norm_fwd(
        mid_stream, full_g2.astype(float_kind), full_s2.astype(float_kind)
    )
    normed_two = h_two.astype(brain_kind)
    pre_act = jnp.dot(normed_two, full_up, preferred_element_type=float_kind) + full_bup.astype(
        float_kind
    )
    hidden = gelu_fwd(pre_act).astype(brain_kind)
    result = (
        mid_stream
        + jnp.dot(hidden, full_down, preferred_element_type=float_kind)
        + full_bdown.astype(float_kind)
    )
    back_params = (
        lax.all_gather(w_qkv, ("seq", "ctx"), axis=0, tiled=True),
        lax.all_gather(b_query, ("seq", "ctx"), axis=0, tiled=True),
        lax.all_gather(b_value, ("seq", "ctx"), axis=0, tiled=True),
        lax.all_gather(w_out, ("seq", "ctx"), axis=0, tiled=True),
        lax.all_gather(b_out, ("seq", "ctx"), axis=0, tiled=True),
        lax.all_gather(gain_one, ("seq", "ctx"), axis=0, tiled=True),
        lax.all_gather(shift_one, ("seq", "ctx"), axis=0, tiled=True),
        lax.all_gather(gain_two, ("seq", "ctx"), axis=0, tiled=True),
        lax.all_gather(shift_two, ("seq", "ctx"), axis=0, tiled=True),
        lax.all_gather(w_up, ("seq", "ctx"), axis=0, tiled=True),
        lax.all_gather(b_up, ("seq", "ctx"), axis=0, tiled=True),
        lax.all_gather(w_down, ("seq", "ctx"), axis=0, tiled=True),
        lax.all_gather(b_down, ("seq", "ctx"), axis=0, tiled=True),
    )
    (
        back_qkv,
        back_bq,
        back_bv,
        back_out,
        back_bout,
        back_g1,
        back_s1,
        back_g2,
        back_s2,
        back_up,
        back_bup,
        back_down,
        back_bdown,
    ) = back_params
    upstream_b = cotangent.reshape(row_count, width)
    upstream = upstream_b.astype(float_kind)
    d_w_down = jnp.dot(hidden.T, upstream_b, preferred_element_type=float_kind)
    d_b_down = jnp.sum(upstream, 0)
    d_hidden = jnp.dot(upstream_b, back_down.T, preferred_element_type=float_kind)
    d_pre = d_hidden * gelu_grad(pre_act)
    d_pre_b = d_pre.astype(brain_kind)
    d_w_up = jnp.dot(normed_two.T, d_pre_b, preferred_element_type=float_kind)
    d_b_up = jnp.sum(d_pre, 0)
    d_normed_two = jnp.dot(d_pre_b, back_up.T, preferred_element_type=float_kind)
    d_mid_norm, d_gain_two, d_shift_two = norm_back(
        d_normed_two, n_two, s_two, back_g2.astype(float_kind)
    )
    d_mid = upstream + d_mid_norm
    d_mid_b = d_mid.astype(brain_kind)
    d_w_out = jnp.dot(attended.T, d_mid_b, preferred_element_type=float_kind)
    d_b_out = jnp.sum(d_mid, 0)
    d_att = jnp.dot(d_mid_b, back_out.T, preferred_element_type=float_kind).astype(brain_kind)
    dq_parts = []
    dk_parts = []
    dv_parts = []
    for group in range(group_count):
        lo_col = group * group_width
        hi_col = lo_col + group_width
        d_query, d_key, d_value = attend_group_back(
            queries[:, lo_col:hi_col],
            keys_all[:, lo_col:hi_col],
            values_all[:, lo_col:hi_col],
            attended[:, lo_col:hi_col],
            d_att[:, lo_col:hi_col],
            totals_parts[group],
            query_pos,
            key_pos,
        )
        dq_parts.append(d_query)
        dk_parts.append(d_key)
        dv_parts.append(d_value)
    d_query = jnp.concatenate(dq_parts, 1)
    key_terms = jnp.concatenate(dk_parts, 1)
    value_terms = jnp.concatenate(dv_parts, 1)
    d_key, d_value = (
        lax.psum_scatter(
            key_terms.astype(jnp.bfloat16), "ctx", scatter_dimension=0, tiled=True
        ).astype(jnp.float32),
        lax.psum_scatter(
            value_terms.astype(jnp.bfloat16), "ctx", scatter_dimension=0, tiled=True
        ).astype(jnp.float32),
    )
    d_proj = jnp.concatenate([d_query, d_key, d_value], 1).astype(brain_kind)
    d_w_qkv = jnp.dot(normed_one.T, d_proj, preferred_element_type=float_kind)
    d_b_query = jnp.sum(d_query, 0)
    d_b_value = jnp.sum(d_value, 0)
    d_normed_one = jnp.dot(d_proj, back_qkv.T, preferred_element_type=float_kind)
    d_in_norm, d_gain_one, d_shift_one = norm_back(
        d_normed_one, n_one, s_one, back_g1.astype(float_kind)
    )
    d_input = d_mid + d_in_norm
    owned = (
        lax.psum_scatter(d_w_qkv, ("seq", "ctx"), scatter_dimension=0, tiled=True),
        lax.psum_scatter(d_b_query, ("seq", "ctx"), scatter_dimension=0, tiled=True),
        lax.psum_scatter(d_b_value, ("seq", "ctx"), scatter_dimension=0, tiled=True),
        lax.psum_scatter(d_w_out, ("seq", "ctx"), scatter_dimension=0, tiled=True),
        lax.psum_scatter(d_b_out, ("seq", "ctx"), scatter_dimension=0, tiled=True),
        lax.psum_scatter(d_gain_one, ("seq", "ctx"), scatter_dimension=0, tiled=True),
        lax.psum_scatter(d_shift_one, ("seq", "ctx"), scatter_dimension=0, tiled=True),
        lax.psum_scatter(d_gain_two, ("seq", "ctx"), scatter_dimension=0, tiled=True),
        lax.psum_scatter(d_shift_two, ("seq", "ctx"), scatter_dimension=0, tiled=True),
        lax.psum_scatter(d_w_up, ("seq", "ctx"), scatter_dimension=0, tiled=True),
        lax.psum_scatter(d_b_up, ("seq", "ctx"), scatter_dimension=0, tiled=True),
        lax.psum_scatter(d_w_down, ("seq", "ctx"), scatter_dimension=0, tiled=True),
        lax.psum_scatter(d_b_down, ("seq", "ctx"), scatter_dimension=0, tiled=True),
    )
    return (
        result.reshape(1, row_count, width).astype(brain_kind),
        d_input.reshape(1, row_count, width),
    ) + tuple(owned)


def xor_send(value, axis, count, mask):
    return lax.ppermute(value, axis, [(i, i ^ mask) for i in range(count)])


def gather_ctx(block, n_ctx):
    far = [block] + [xor_send(block, "ctx", n_ctx, 2 * k) for k in range(1, n_ctx // 2)]
    out = []
    for piece in far:
        out += [piece, xor_send(piece, "ctx", n_ctx, 1)]
    return out


def reduce_ctx(blocks, n_ctx):
    half = n_ctx // 2
    sums = [None] * half
    for k in list(range(1, half)) + [0]:
        other = xor_send(blocks[2 * k + 1].astype(jnp.bfloat16), "ctx", n_ctx, 1)
        sums[k] = blocks[2 * k].astype(jnp.float32) + other.astype(jnp.float32)
    total = sums[0]
    for k in range(1, half):
        total = total + xor_send(sums[k].astype(jnp.bfloat16), "ctx", n_ctx, 2 * k).astype(
            jnp.float32
        )
    return total


def gather_seq(block, n_seq):
    return [block] + [xor_send(block, "seq", n_seq, j) for j in range(1, n_seq)]


def reduce_seq(blocks, n_seq):
    total = blocks[0].astype(jnp.float32)
    for j in range(1, n_seq):
        total = total + xor_send(blocks[j].astype(jnp.bfloat16), "seq", n_seq, j).astype(
            jnp.float32
        )
    return total


def xor_order(blocks, index):
    step = 1
    while step < len(blocks):
        bit = (index // step) % 2 == 1
        blocks = [jnp.where(bit, blocks[i ^ step], blocks[i]) for i in range(len(blocks))]
        step *= 2
    return blocks


def one_hot(columns, width):
    return (columns[:, None] == jnp.arange(width, dtype=jnp.int32)[None, :]).astype(jnp.bfloat16)


def dot(a, b, precision=None):
    return jnp.dot(a, b, preferred_element_type=jnp.float32, precision=precision)


def dot_nt(a, b, precision=None):
    return lax.dot_general(
        a, b, (((1,), (1,)), ((), ())), preferred_element_type=jnp.float32, precision=precision
    )


def dot_tn(a, b):
    return lax.dot_general(a, b, (((0,), (0,)), ((), ())), preferred_element_type=jnp.float32)


def masked_scores(q3, k3, query_pos, key_pos):
    scores = jnp.einsum("bqd,bkd->bqk", q3, k3, preferred_element_type=jnp.float32) * 0.125
    causal = key_pos[None, None, :] <= query_pos[:, :, None]
    return jnp.where(causal, scores, -1e30)


def attend(q3, k3, v3, query_pos, key_pos):
    scores = masked_scores(q3, k3, query_pos, key_pos)
    row_max = jnp.max(scores, -1, keepdims=True)
    log_total = row_max + jnp.log(jnp.sum(jnp.exp(scores - row_max), -1, keepdims=True))
    weights = jnp.exp(scores - log_total).astype(jnp.bfloat16)
    att = jnp.einsum("bqk,bkd->bqd", weights, v3, preferred_element_type=jnp.float32)
    return att.astype(jnp.bfloat16), log_total


def attend_back(q3, k3, v3, att3, d3, log_total, query_pos, key_pos):
    scores = masked_scores(q3, k3, query_pos, key_pos)
    probs = jnp.exp(scores - log_total)
    weights = probs.astype(jnp.bfloat16)
    delta = jnp.sum(d3.astype(jnp.float32) * att3.astype(jnp.float32), -1, keepdims=True)
    d_prob = jnp.einsum("bqd,bkd->bqk", d3, v3, preferred_element_type=jnp.float32)
    d_score = (0.125 * probs * (d_prob - delta)).astype(jnp.bfloat16)
    d_q = jnp.einsum("bqk,bkd->bqd", d_score, k3, preferred_element_type=jnp.float32)
    d_k = jnp.einsum("bqk,bqd->bkd", d_score, q3, preferred_element_type=jnp.float32)
    d_v = jnp.einsum("bqk,bqd->bkd", weights, d3, preferred_element_type=jnp.float32)
    return d_q, d_k, d_v


def split_device(
    n_seq,
    n_ctx,
    block_input,
    w_qkv,
    b_query,
    b_value,
    w_out,
    b_out,
    gain_one,
    shift_one,
    gain_two,
    shift_two,
    w_up,
    b_up,
    w_down,
    b_down,
    cotangent,
):
    f32 = jnp.float32
    bf = jnp.bfloat16
    n_dev = n_seq * n_ctx
    rows = block_input.shape[1]
    width = block_input.shape[2]
    heads = width // HD
    own = width // n_dev
    tp_hidden = w_up.shape[1] // n_seq
    up_own = b_up.shape[0]
    per = up_own // own
    half_rows = rows // 2
    s = lax.axis_index("seq")
    c = lax.axis_index("ctx")
    odd = c % 2

    x_own = block_input.reshape(rows, width)
    cot_own = cotangent.reshape(rows, width)
    x_all = jnp.concatenate(gather_ctx(x_own, n_ctx), 0)

    slab = jnp.concatenate(
        [
            v.reshape(1, own)
            for v in (b_query, b_value, b_out, gain_one, shift_one, gain_two, shift_two, b_down)
        ]
        + [b_up.reshape(per, own)],
        0,
    ).T
    n_vec = 8 + per
    slab = jnp.pad(slab, ((0, 0), (0, 128 - n_vec)))
    w4 = w_qkv.reshape(own, 3, heads, HD)
    full_w = w4[:, :, :n_ctx]
    part_w = jnp.repeat(w4[:, :, n_ctx:], 2, axis=2)
    to_heads = jnp.stack([full_w, part_w], 3).transpose(2, 0, 1, 3, 4).reshape(n_ctx, own, 6 * HD)
    to_heads = jnp.concatenate([to_heads, jnp.broadcast_to(slab[None], (n_ctx, own, 128))], 2)
    from_ctx = lax.all_to_all(to_heads, "ctx", 0, 0, tiled=True)
    from_ctx = from_ctx.reshape(n_ctx * own, 6 * HD + 128)
    head_w = jnp.concatenate(xor_order(gather_seq(from_ctx, n_seq), s), 0)
    vectors = head_w[:, 6 * HD : 6 * HD + n_vec].T.astype(f32)
    head_w = head_w[:, : 6 * HD]
    bq, bv, bo, g1, s1, g2, s2, bd = [vectors[k][None] for k in range(8)]

    cot_all = jnp.concatenate(gather_seq(cot_own, n_seq), 0)

    up_rows = lax.all_to_all(
        w_up.reshape(own, n_seq, tp_hidden).transpose(1, 0, 2), "seq", 0, 0, tiled=True
    ).reshape(n_seq * own, tp_hidden)
    up_rel = jnp.concatenate(gather_ctx(up_rows, n_ctx), 0)
    down_rel = jnp.concatenate(gather_ctx(w_down, n_ctx), 0)

    far = [w_out] + [xor_send(w_out, "ctx", n_ctx, 2 * k) for k in range(1, n_ctx // 2)]
    out_z = jnp.stack(far, 0)
    out_y = jnp.stack([out_z, xor_send(out_z, "ctx", n_ctx, 1)], 1).reshape(n_ctx * own, width)
    mask = n_seq // 2
    out_g = out_y[None]
    while mask >= 1:
        out_g = jnp.concatenate([out_g[None], xor_send(out_g, "seq", n_seq, mask)[None]], 0)
        mask //= 2
    bits = out_g.ndim - 3
    out_g = out_g.transpose(tuple(range(bits - 1, -1, -1)) + (bits, bits + 1, bits + 2))
    out_g = out_g.reshape(width, width)

    feat = jnp.arange(width, dtype=jnp.int32)
    f_dev = feat // own
    f_s = f_dev // n_ctx
    f_c = f_dev % n_ctx
    f_i = feat % own
    to_up = one_hot((f_c ^ c) * (n_seq * own) + f_s * own + f_i, width)
    hid = jnp.arange(tp_hidden, dtype=jnp.int32)
    to_hid = one_hot(((hid // up_own) ^ c) * up_own + hid % up_own, tp_hidden)
    rel_head = feat // HD
    canon_head = jnp.where(rel_head < n_ctx, rel_head ^ c, n_ctx + ((rel_head - n_ctx) ^ (c // 2)))
    canon_row = canon_head * HD + feat % HD
    r_dev = canon_row // own
    to_out = one_hot(
        (((r_dev // n_ctx) ^ s) * n_ctx + ((r_dev % n_ctx) ^ c)) * own + canon_row % own, width
    )
    out_rel = dot(to_out, out_g).astype(bf)
    up_p = dot(up_rel, to_hid).astype(bf)
    bup = vectors[8:].reshape(per, n_seq, n_ctx, own)
    bup = lax.dynamic_index_in_dim(bup, s, 1, keepdims=False).transpose(1, 0, 2)
    bup = dot(bup.reshape(1, tp_hidden).astype(bf), to_hid)

    x_float = x_all.astype(f32)
    h_one, n_one, sc_one = norm_fwd(x_float, g1, s1)
    normed_one = h_one.astype(bf)
    proj = dot(normed_one, head_w)
    length = proj.shape[0]

    def head_bias(vec):
        return jnp.concatenate(
            [
                lax.dynamic_slice(vec[0], (c * HD,), (HD,)),
                lax.dynamic_slice(vec[0], ((n_ctx + c // 2) * HD,), (HD,)),
            ]
        )[None]

    q2 = (proj[:, : 2 * HD] + head_bias(bq)).astype(bf)
    k2 = proj[:, 2 * HD : 4 * HD].astype(bf)
    v2 = (proj[:, 4 * HD :] + head_bias(bv)).astype(bf)

    def by_half(arr):
        return arr.reshape(n_ctx, 2, half_rows, HD).transpose(1, 0, 2, 3).reshape(2, length // 2, HD)

    def pick_half(arr):
        return lax.dynamic_index_in_dim(by_half(arr), odd, 0, keepdims=True)

    q3 = jnp.concatenate([by_half(q2[:, :HD]), pick_half(q2[:, HD:])], 0)
    k3 = jnp.stack([k2[:, :HD], k2[:, :HD], k2[:, HD:]], 0)
    v3 = jnp.stack([v2[:, :HD], v2[:, :HD], v2[:, HD:]], 0)
    token = jnp.arange(length, dtype=jnp.int32)
    key_pos = ((token // rows) ^ c) * rows + token % rows
    pos2 = key_pos.reshape(n_ctx, 2, half_rows).transpose(1, 0, 2).reshape(2, length // 2)
    query_pos = jnp.concatenate([pos2, lax.dynamic_index_in_dim(pos2, odd, 0)], 0)
    att3, log_total = attend(q3, k3, v3, query_pos, key_pos)

    def swap_ctx(payload):
        return jnp.stack(
            [payload[0]] + [xor_send(payload[r], "ctx", n_ctx, r) for r in range(1, n_ctx)], 0
        )

    sent = att3.reshape(3, n_ctx, half_rows, HD).transpose(1, 2, 0, 3)
    got = swap_ctx(sent.reshape(n_ctx, half_rows, 3 * HD)).reshape(n_ctx, half_rows, 3, HD)
    att_full = got[:, :, :2].transpose(2, 1, 0, 3).reshape(rows, n_ctx * HD)
    att_part = got[:, :, 2].reshape(n_ctx // 2, 2, half_rows, HD)
    att_part = jnp.where(odd == 1, att_part[:, ::-1], att_part)
    att_part = att_part.transpose(1, 2, 0, 3).reshape(rows, n_ctx // 2 * HD)
    attended = jnp.concatenate([att_full, att_part], 1)

    mid_stream = x_own.astype(f32) + dot(attended, out_rel) + bo
    h_two, n_two, sc_two = norm_fwd(mid_stream, g2, s2)
    normed_two = dot(h_two.astype(bf), to_up).astype(bf)

    two_all = jnp.concatenate(gather_seq(normed_two, n_seq), 0)
    pre_act = dot(two_all, up_p) + bup
    hidden = gelu_fwd(pre_act).astype(bf)
    d_hidden = dot_nt(cot_all, down_rel)
    d_pre = d_hidden * gelu_grad(pre_act)
    d_pre_b = d_pre.astype(bf)
    d_two = dot_nt(d_pre_b, up_p).astype(bf).reshape(n_seq, rows, width)
    d_two = reduce_seq([d_two[j] for j in range(n_seq)], n_seq)
    d_normed_two = dot_nt(d_two, to_up.astype(f32), precision=lax.Precision.HIGHEST)

    out_part = dot(hidden, down_rel).reshape(n_seq, rows, width)
    result = mid_stream + reduce_seq([out_part[j] for j in range(n_seq)], n_seq) + bd

    d_w_down = dot_tn(hidden, cot_all).astype(bf)
    d_b_up = jnp.sum(d_pre, 0).astype(bf)
    d_down_ext = jnp.concatenate(
        [d_w_down, jnp.pad(d_b_up[:, None], ((0, 0), (0, 127)))], 1
    ).reshape(n_ctx, up_own, width + 128)
    d_down = reduce_ctx([d_down_ext[r] for r in range(n_ctx)], n_ctx)
    d_pre_canon = dot_nt(d_pre_b, to_hid).astype(bf)
    d_w_up = dot_tn(two_all, d_pre_canon).astype(bf).reshape(n_ctx, n_seq * own, tp_hidden)
    d_up = reduce_ctx([d_w_up[r] for r in range(n_ctx)], n_ctx).astype(bf)
    d_up = lax.all_to_all(d_up.reshape(n_seq, own, tp_hidden), "seq", 0, 0, tiled=True)
    d_up = d_up.transpose(1, 0, 2).reshape(own, n_seq * tp_hidden).astype(f32)

    upstream = cot_own.astype(f32)
    d_mid_norm, d_gain_two, d_shift_two = norm_back(d_normed_two, n_two, sc_two, g2)
    d_mid = upstream + d_mid_norm
    d_mid_b = d_mid.astype(bf)
    d_att = dot_nt(d_mid_b, out_rel).astype(bf)
    d_full = d_att[:, : n_ctx * HD].reshape(2, half_rows, n_ctx, HD).transpose(2, 1, 0, 3)
    d_part = d_att[:, n_ctx * HD :].reshape(2, half_rows, n_ctx // 2, HD).transpose(2, 0, 1, 3)
    d_part = jnp.where(odd == 1, d_part[:, ::-1], d_part).reshape(n_ctx, half_rows, 1, HD)
    d_sent = jnp.concatenate([d_full, d_part], 2).reshape(n_ctx, half_rows, 3 * HD)
    d3 = swap_ctx(d_sent).reshape(n_ctx, half_rows, 3, HD).transpose(2, 0, 1, 3)
    d3 = d3.reshape(3, length // 2, HD)

    d_w_out = lax.dot_general(
        to_out, dot_tn(attended, d_mid_b).astype(bf), (((0,), (0,)), ((), ())),
        preferred_element_type=f32,
    ).astype(bf)
    part = d_w_out.reshape(n_seq, n_ctx, own, width)
    mask = 1
    while part.shape[0] > 1:
        pair = part.reshape(part.shape[0] // 2, 2, n_ctx, own, width)
        other = xor_send(pair[:, 1], "seq", n_seq, mask)
        part = (pair[:, 0].astype(f32) + other.astype(f32)).astype(bf)
        mask *= 2
    part = part.reshape(n_ctx // 2, 2, own, width)
    part = part[:, 0].astype(f32) + xor_send(part[:, 1], "ctx", n_ctx, 1).astype(f32)
    d_out = part[0]
    for k in range(1, n_ctx // 2):
        d_out = d_out + xor_send(part[k].astype(bf), "ctx", n_ctx, 2 * k).astype(f32)

    d_q, d_k, d_v = attend_back(q3, k3, v3, att3, d3, log_total, query_pos, key_pos)

    def un_half(arr):
        return arr.reshape(2, n_ctx, half_rows, HD).transpose(1, 0, 2, 3).reshape(length, HD)

    dq_part = jnp.where(jnp.arange(2)[:, None, None] == odd, d_q[2:3], 0.0)
    d_proj = jnp.concatenate(
        [
            un_half(d_q[:2]),
            un_half(dq_part),
            d_k[0] + d_k[1],
            d_k[2],
            d_v[0] + d_v[1],
            d_v[2],
        ],
        1,
    )
    d_proj_b = d_proj.astype(bf)
    d_one_part = dot_nt(d_proj_b, head_w)
    d_one_blocks = d_one_part.reshape(n_ctx, rows, width)
    d_normed_one = reduce_ctx([d_one_blocks[r] for r in range(n_ctx)], n_ctx)
    grad_in, _, _ = norm_back(d_normed_one, n_one[:rows], sc_one[:rows], g1)
    d_input = d_mid + grad_in

    col_sum = jnp.sum(d_proj, 0)

    def place(lo):
        zero = jnp.zeros((width,), f32)
        zero = lax.dynamic_update_slice(zero, col_sum[lo : lo + HD], (c * HD,))
        return lax.dynamic_update_slice(
            zero, col_sum[lo + HD : lo + 2 * HD], ((n_ctx + c // 2) * HD,)
        )

    vec_grads = jnp.stack(
        [
            place(0),
            place(4 * HD),
            jnp.sum(d_mid, 0),
            jnp.sum(d_one_part * n_one, 0),
            jnp.sum(d_one_part, 0),
            d_gain_two,
            d_shift_two,
            jnp.sum(upstream, 0),
        ],
        1,
    )
    d_heads = jnp.concatenate(
        [dot_tn(normed_one, d_proj_b), jnp.pad(vec_grads, ((0, 0), (0, 120)))], 1
    ).astype(bf)
    d_heads = lax.all_to_all(
        d_heads.reshape(n_seq, n_ctx * own, 6 * HD + 128), "seq", 0, 0, tiled=True
    )
    d_heads = jnp.sum(d_heads.astype(f32), 0).astype(bf)
    d_heads = lax.all_to_all(
        d_heads.reshape(n_ctx, own, 6 * HD + 128), "ctx", 0, 0, tiled=True
    ).astype(f32)
    vec_out = jnp.sum(d_heads[:, :, 6 * HD : 6 * HD + 8], 0)
    d_cols = d_heads[:, :, : 6 * HD].reshape(n_ctx, own, 3, 2, HD)
    d_first = d_cols[:, :, :, 0].transpose(1, 2, 0, 3)
    d_rest = d_cols[:, :, :, 1].reshape(n_ctx // 2, 2, own, 3, HD).sum(1).transpose(1, 2, 0, 3)
    d_w_qkv = jnp.concatenate([d_first, d_rest], 2).reshape(own, 3 * width)

    return (
        result.reshape(1, rows, width).astype(bf),
        d_input.reshape(1, rows, width),
        d_w_qkv,
        vec_out[:, 0],
        vec_out[:, 1],
        d_out,
        vec_out[:, 2],
        vec_out[:, 3],
        vec_out[:, 4],
        vec_out[:, 5],
        vec_out[:, 6],
        d_up,
        d_down[:, width],
        d_down[:, :width],
        vec_out[:, 7],
    )


def pick_plan(mesh):
    n_seq = mesh.shape["seq"]
    n_ctx = mesh.shape["ctx"]

    def per_device(*args):
        width = args[0].shape[2]
        heads = width // HD
        hidden = args[10].shape[1]
        fits = (
            n_seq & (n_seq - 1) == 0
            and n_ctx & (n_ctx - 1) == 0
            and 2 * (heads - n_ctx) == n_ctx
            and width % (n_seq * n_ctx) == 0
            and hidden % width == 0
            and args[0].shape[1] % 2 == 0
        )
        if fits:
            return split_device(n_seq, n_ctx, *args)
        return general_device(*args)

    return per_device


def solution(mesh):
    placed = (
        P("seq", "ctx", None),
        P(("seq", "ctx"), None),
        P(("seq", "ctx")),
        P(("seq", "ctx")),
        P(("seq", "ctx"), None),
        P(("seq", "ctx")),
        P(("seq", "ctx")),
        P(("seq", "ctx")),
        P(("seq", "ctx")),
        P(("seq", "ctx")),
        P(("seq", "ctx"), None),
        P(("seq", "ctx")),
        P(("seq", "ctx"), None),
        P(("seq", "ctx")),
        P("seq", "ctx", None),
    )
    return jax.shard_map(
        pick_plan(mesh),
        mesh=mesh,
        in_specs=placed,
        out_specs=(
            P("seq", "ctx", None),
            P("seq", "ctx", None),
            P(("seq", "ctx"), None),
            P(("seq", "ctx")),
            P(("seq", "ctx")),
            P(("seq", "ctx"), None),
            P(("seq", "ctx")),
            P(("seq", "ctx")),
            P(("seq", "ctx")),
            P(("seq", "ctx")),
            P(("seq", "ctx")),
            P(("seq", "ctx"), None),
            P(("seq", "ctx")),
            P(("seq", "ctx"), None),
            P(("seq", "ctx")),
        ),
        check_vma=False,
    )
```
